32 devices in a mesh: view: 8 (over z, core), head: 4 (over y, x).
Axes of the slice: x: 2, y: 2, z: 4, core: 2. Of those that a mesh axis runs over, the one named last changes fastest.
Arguments:
- tokens: bfloat16 [16, 512, 1024], P('view', 'head'), may hold values from -6 to 6
- w_qkv_frame: bfloat16 [1024, 3072], replicated, may hold values from -2 to 2
- w_out_frame: bfloat16 [1024, 1024], replicated, may hold values from -0.1875 to 0.1875
- w_qkv_global: bfloat16 [1024, 3072], replicated, may hold values from -2 to 2
- w_out_global: bfloat16 [1024, 1024], replicated, may hold values from -0.1875 to 0.1875
Outputs:
- result: bfloat16 [16, 512, 1024], P('view', 'head')
The draws below stay inside these ranges and needn't reach their ends.
All inputs are finite; a program needn't handle non-finite values.
Results may differ from the reference program's by a relative error of at most 0.012.
Values may be sent and summed in bfloat16 or wider, within the bound.
A program may use at most 128 MiB of HBM per device.

```python
import math
import jax
import jax.numpy as jnp
from jax import lax

D = 1024
HEADS = 16
HEAD = 64
TOK = 512
VIEWS = 16


def qkv_table(key):
    column_scale = 1.7 / math.sqrt(D)
    key_query = jax.random.fold_in(key, 0)
    table = jax.random.normal(key_query, (D, 3 * D), jnp.float32) * column_scale
    return jnp.clip(table, -2.0, 2.0).astype(jnp.bfloat16)


def draw_w_qkv_frame(key, part):
    return qkv_table(jax.random.fold_in(key, 11))


def draw_w_qkv_global(key, part):
    return qkv_table(jax.random.fold_in(key, 23))


def steps_of(key, extent, cuts, least, largest):
    factor_of, own = 1.0, jax.random.fold_in(key, 6)
    for position, parts in cuts:
        heights = jnp.exp(jax.random.uniform(jax.random.fold_in(own, position), (parts,), jnp.float32, least / len(cuts), largest / len(cuts)))
        factor_of = factor_of * jnp.repeat(heights, extent[position] // parts).reshape([-1 if axis == position else 1 for axis in range(len(extent))])
    return factor_of


def normal_values(stream_key, extent, deviation, reach, pieces=(), held_as=jnp.bfloat16):
    array = deviation * jax.random.normal(stream_key, extent, jnp.float32)
    if pieces:
        array = array * steps_of(stream_key, extent, pieces, -0.22, 0.18)
    return jnp.clip(array, -reach, reach).astype(held_as)


def setup_inputs(seed: int = 0) -> dict:
    keys = jax.random.split(jax.random.key(seed), 6)
    return {
        "tokens": normal_values(keys[0], (VIEWS, TOK, D), 1.0, 6.0, ((0, 8), (1, 4))),
        "w_qkv_frame": draw_w_qkv_frame(jax.random.fold_in(keys[5], 71), 0),
        "w_out_frame": normal_values(keys[2], (D, D), D ** -0.5, 0.1875),
        "w_qkv_global": draw_w_qkv_global(jax.random.fold_in(keys[5], 71), 0),
        "w_out_global": normal_values(keys[4], (D, D), D ** -0.5, 0.1875),
    }


def normalize(stream):
    widened = stream.astype(jnp.float32)
    center = lax.optimization_barrier(jnp.mean(widened, axis=-1, keepdims=True))
    spread = lax.optimization_barrier(jnp.mean(jnp.square(widened - center), axis=-1, keepdims=True))
    return ((widened - center) * lax.rsqrt(spread + 1e-06)).astype(jnp.bfloat16)

def project_qkv(stream, weight):
    normed = normalize(stream).reshape(VIEWS * TOK, D)
    packed = jnp.dot(normed, weight, preferred_element_type=jnp.float32).astype(jnp.bfloat16)
    return packed.reshape(VIEWS * TOK, 3, HEADS, HEAD)

def attend(queries, keys_all, values_all):
    scores = jnp.dot(queries, keys_all.T, preferred_element_type=jnp.float32) * HEAD ** (-0.5)
    top_score = lax.optimization_barrier(jnp.max(scores, axis=-1, keepdims=True))
    exp_terms = jnp.exp(scores - top_score)
    row_sum = lax.optimization_barrier(jnp.sum(exp_terms, axis=-1, keepdims=True))
    shares = exp_terms.astype(jnp.bfloat16)
    return jnp.dot(shares, values_all, preferred_element_type=jnp.float32) / row_sum

def frame_view(packed):
    mixed_out = jax.vmap(attend, in_axes=(1, 1, 1), out_axes=1)(packed[:, 0], packed[:, 1], packed[:, 2])
    return mixed_out.astype(jnp.bfloat16).reshape(TOK, D)

def reference(tokens, w_qkv_frame, w_out_frame, w_qkv_global, w_out_global):
    packed_frame = project_qkv(tokens, w_qkv_frame).reshape(VIEWS, TOK, 3, HEADS, HEAD)
    frame_mixed = lax.map(frame_view, packed_frame)
    added_frame = jnp.dot(frame_mixed.reshape(VIEWS * TOK, D), w_out_frame, preferred_element_type=jnp.float32)
    after_frame = (tokens.astype(jnp.float32) + added_frame.reshape(VIEWS, TOK, D)).astype(jnp.bfloat16)
    packed_global = project_qkv(after_frame, w_qkv_global)

    def one_head(head_id):
        query_head = packed_global[:, 0, head_id]
        key_head = packed_global[:, 1, head_id]
        value_head = packed_global[:, 2, head_id]
        blocks_out = lax.map(lambda qblock: attend(qblock, key_head, value_head).astype(jnp.bfloat16), query_head.reshape(VIEWS, TOK, HEAD))
        return blocks_out
    per_head = lax.map(one_head, jnp.arange(HEADS, dtype=jnp.int32))
    global_mixed = jnp.transpose(per_head, (1, 2, 0, 3)).reshape(VIEWS * TOK, D)
    added_global = jnp.dot(global_mixed, w_out_global, preferred_element_type=jnp.float32)
    return (after_frame.astype(jnp.float32) + added_global.reshape(VIEWS, TOK, D)).astype(jnp.bfloat16)
```

```python
import functools
import math

import jax
import jax.numpy as jnp
from jax import lax
from jax.experimental import pallas as pl
from jax.experimental.pallas import tpu as pltpu
from jax.sharding import PartitionSpec as P

HEAD = 64
LANES = 128
SCORE_SCALE = HEAD ** (-0.5) * math.log2(math.e)
VMEM_BYTES = 56 * 2**20


def normalize(stream):
    widened = stream.astype(jnp.float32)
    center = jnp.mean(widened, axis=-1, keepdims=True)
    spread = jnp.mean(jnp.square(widened - center), axis=-1, keepdims=True)
    return ((widened - center) * lax.rsqrt(spread + 1e-06)).astype(jnp.bfloat16)


def frame_kernel(q_ref, k_ref, v_ref, o_ref):
    outs = []
    for head in range(q_ref.shape[1] // HEAD):
        cols = slice(head * HEAD, (head + 1) * HEAD)
        scores = lax.dot_general(
            q_ref[:, cols], k_ref[:, cols], (((1,), (1,)), ((), ())),
            preferred_element_type=jnp.float32,
        )
        terms = jnp.exp2(scores - jnp.max(scores, axis=1, keepdims=True))
        total = jnp.sum(terms, axis=1, keepdims=True)
        mixed = jnp.dot(
            terms.astype(jnp.bfloat16), v_ref[:, cols], preferred_element_type=jnp.float32
        )
        outs.append(mixed / total)
    o_ref[...] = jnp.concatenate(outs, axis=1).astype(jnp.bfloat16)


def frame_attention(queries, keys, values):
    rows, cols = queries.shape
    spec = pl.BlockSpec((rows, LANES), lambda i: (0, i))
    return pl.pallas_call(
        frame_kernel,
        grid=(cols // LANES,),
        in_specs=[spec] * 3,
        out_specs=spec,
        out_shape=jax.ShapeDtypeStruct((rows, cols), jnp.bfloat16),
        compiler_params=pltpu.CompilerParams(vmem_limit_bytes=VMEM_BYTES),
        name="frame_attention",
    )(queries, keys, values)


def global_kernel(key_step, q_ref, kv_ref, o_ref, keys, values):
    pieces, _, head, width = kv_ref.shape

    @pl.when(pl.program_id(0) == 0)
    def _():
        def lay_out(piece, carry):
            at = pl.ds(pl.multiple_of(piece * width, width), width)
            keys[:, at] = kv_ref[piece, 0]
            wide = jnp.concatenate(
                [kv_ref[piece, 1], jnp.ones((LANES - head, width), jnp.bfloat16)], axis=0
            )
            values[at, :] = wide.T
            return carry

        lax.fori_loop(0, pieces, lay_out, 0)

    blocks = q_ref.shape[0]
    queries = jnp.concatenate([q_ref[i, 0] for i in range(blocks)], axis=1).T
    rows = queries.shape[0]
    peak = jnp.full((rows, 1), -1e30, jnp.float32)
    accum = jnp.zeros((rows, LANES), jnp.float32)
    for start in range(0, pieces * width, key_step):
        scores = jnp.dot(
            queries, keys[:, start : start + key_step], preferred_element_type=jnp.float32
        )
        peak_new = jnp.maximum(peak, jnp.max(scores, axis=1, keepdims=True))
        terms = jnp.exp2(scores - peak_new).astype(jnp.bfloat16)
        accum = accum * jnp.exp2(peak - peak_new) + jnp.dot(
            terms, values[start : start + key_step, :], preferred_element_type=jnp.float32
        )
        peak = peak_new
    mixed = (accum[:, :head] / accum[:, head : head + 1]).T.astype(jnp.bfloat16)
    for i in range(blocks):
        o_ref[i] = mixed[:, i * width : (i + 1) * width]


def global_attention(packed, key_values, query_step, key_step):
    sources, _, head, width = packed.shape
    pieces = key_values.shape[0]
    blocks = min(sources, max(1, query_step // width))
    key_step = min(key_step, pieces * width)
    return pl.pallas_call(
        functools.partial(global_kernel, key_step),
        grid=(sources // blocks,),
        in_specs=[
            pl.BlockSpec((blocks, 1, head, width), lambda i: (i, 0, 0, 0)),
            pl.BlockSpec((pieces, 2, head, width), lambda i: (0, 0, 0, 0)),
        ],
        out_specs=pl.BlockSpec((blocks, head, width), lambda i: (i, 0, 0)),
        out_shape=jax.ShapeDtypeStruct((sources, head, width), jnp.bfloat16),
        scratch_shapes=[
            pltpu.VMEM((head, pieces * width), jnp.bfloat16),
            pltpu.VMEM((pieces * width, LANES), jnp.bfloat16),
        ],
        compiler_params=pltpu.CompilerParams(vmem_limit_bytes=VMEM_BYTES),
        name="global_attention",
    )(packed, key_values)


def on_device(tokens, w_qkv_frame, w_out_frame, w_qkv_global, w_out_global):
    view_here, rows_here, model_dim = tokens.shape
    head_size, view_size = lax.axis_size("head"), lax.axis_size("view")
    tokens_here = view_here * rows_here

    shares = head_size // view_here
    cols = model_dim // shares
    share = lax.rem(lax.axis_index("head"), shares)
    sent = jnp.repeat(normalize(tokens), shares, axis=0)
    view_rows = lax.all_to_all(sent, "head", split_axis=0, concat_axis=0, tiled=True)
    view_rows = view_rows.reshape(head_size * rows_here, model_dim)

    def project(which):
        weight = lax.dynamic_slice_in_dim(w_qkv_frame, which * model_dim + share * cols, cols, 1)
        return jnp.dot(view_rows, weight, preferred_element_type=jnp.float32)

    frame_mixed = frame_attention(
        (project(0) * SCORE_SCALE).astype(jnp.bfloat16),
        project(1).astype(jnp.bfloat16),
        project(2).astype(jnp.bfloat16),
    )
    back = lax.all_to_all(
        frame_mixed.reshape(head_size, rows_here, cols), "head", split_axis=0, concat_axis=0, tiled=True
    ).reshape(view_here, shares, rows_here, cols)
    added = jnp.dot(
        jnp.transpose(back, (0, 2, 1, 3)).reshape(tokens_here, model_dim),
        w_out_frame,
        preferred_element_type=jnp.float32,
    )
    after_frame = (tokens.astype(jnp.float32).reshape(tokens_here, model_dim) + added).astype(
        jnp.bfloat16
    )

    heads = model_dim // HEAD
    copies = view_size * head_size // heads
    normed = normalize(after_frame)
    packed = lax.dot_general(
        w_qkv_global, normed, (((0,), (1,)), ((), ())), preferred_element_type=jnp.float32
    ).reshape(3, heads, HEAD, tokens_here)
    scale = jnp.array([SCORE_SCALE, 1.0, 1.0], jnp.float32).reshape(3, 1, 1, 1)
    packed = jnp.transpose((packed * scale).astype(jnp.bfloat16), (1, 0, 2, 3))
    groups = [
        [
            (outer * copies + copy) * head_size + inner
            for outer in range(view_size // copies)
            for inner in range(head_size)
        ]
        for copy in range(copies)
    ]
    by_head = lax.all_to_all(
        packed, ("view", "head"), split_axis=0, concat_axis=0, axis_index_groups=groups, tiled=True
    )
    key_values = lax.all_gather(
        by_head[:, 1:],
        "view",
        axis=0,
        axis_index_groups=[
            [outer * copies + copy for copy in range(copies)]
            for outer in range(view_size // copies)
        ],
        tiled=True,
    )
    mixed = global_attention(by_head, key_values, 1024, 1024)
    mixed = lax.all_to_all(
        mixed, ("view", "head"), split_axis=0, concat_axis=0, axis_index_groups=groups, tiled=True
    ).reshape(model_dim, tokens_here)
    added = lax.dot_general(
        mixed, w_out_global, (((0,), (0,)), ((), ())), preferred_element_type=jnp.float32
    )
    result = (after_frame.astype(jnp.float32) + added).astype(jnp.bfloat16)
    return result.reshape(view_here, rows_here, model_dim)


def solution(mesh):
    return jax.shard_map(
        on_device,
        mesh=mesh,
        in_specs=(P("view", "head", None), P(), P(), P(), P()),
        out_specs=P("view", "head", None),
        check_vma=False,
    )
```

```python
import functools
import math

import jax
import jax.numpy as jnp
from jax import lax
from jax.experimental import pallas as pl
from jax.experimental.pallas import tpu as pltpu
from jax.sharding import PartitionSpec as P

HEAD = 64
LANES = 128
SCORE_SCALE = HEAD ** (-0.5) * math.log2(math.e)
VMEM_BYTES = 56 * 2**20


def normalize(stream):
    widened = stream.astype(jnp.float32)
    center = jnp.mean(widened, axis=-1, keepdims=True)
    spread = jnp.mean(jnp.square(widened - center), axis=-1, keepdims=True)
    return ((widened - center) * lax.rsqrt(spread + 1e-06)).astype(jnp.bfloat16)


def frame_kernel(q_ref, k_ref, v_ref, o_ref):
    outs = []
    for head in range(q_ref.shape[1] // HEAD):
        cols = slice(head * HEAD, (head + 1) * HEAD)
        scores = lax.dot_general(
            q_ref[:, cols], k_ref[:, cols], (((1,), (1,)), ((), ())),
            preferred_element_type=jnp.float32,
        )
        terms = jnp.exp2(scores - jnp.max(scores, axis=1, keepdims=True))
        total = jnp.sum(terms, axis=1, keepdims=True)
        mixed = jnp.dot(
            terms.astype(jnp.bfloat16), v_ref[:, cols], preferred_element_type=jnp.float32
        )
        outs.append(mixed / total)
    o_ref[...] = jnp.concatenate(outs, axis=1).astype(jnp.bfloat16)


def frame_attention(queries, keys, values):
    rows, cols = queries.shape
    spec = pl.BlockSpec((rows, LANES), lambda i: (0, i))
    return pl.pallas_call(
        frame_kernel,
        grid=(cols // LANES,),
        in_specs=[spec] * 3,
        out_specs=spec,
        out_shape=jax.ShapeDtypeStruct((rows, cols), jnp.bfloat16),
        compiler_params=pltpu.CompilerParams(vmem_limit_bytes=VMEM_BYTES),
        name="frame_attention",
    )(queries, keys, values)


def global_kernel(
    planes, copies, per_plane, key_step,
    packed, out_ref,
    got_q, got_kv, keys, values, peaks, accums, out_buf,
    q_send, q_recv, kv_send, kv_recv, on_send, on_recv, out_send, out_recv,
):
    _, _, head, width = packed.shape
    view, spot = lax.axis_index("view"), lax.axis_index("head")
    plane, copy = view // copies, lax.rem(view, copies)
    mine = plane * per_plane + spot
    stage_rows = per_plane * width

    def device(to_plane, to_copy, to_spot):
        return (to_plane * copies + to_copy, to_spot)

    def remote(src, dst, send, recv, target):
        return pltpu.make_async_remote_copy(
            src_ref=src, dst_ref=dst, send_sem=send, recv_sem=recv,
            device_id=target, device_id_type=pl.DeviceIdType.MESH,
        )

    def q_copy(stage, step):
        to_plane, to_spot = lax.rem(plane + stage, planes), lax.rem(spot + step, per_plane)
        slot, order = stage * per_plane + spot, stage * per_plane + step
        return remote(
            packed.at[to_plane * per_plane + to_spot, 0], got_q.at[slot],
            q_send.at[order], q_recv.at[slot], device(to_plane, copy, to_spot),
        )

    def kv_copy(stage, step):
        to_plane, to_spot = lax.rem(plane + stage, planes), lax.rem(spot + step, per_plane)
        slot, order = stage * per_plane + spot, stage * per_plane + step
        return remote(
            packed.at[to_plane * per_plane + to_spot, pl.ds(1, 2)], got_kv.at[0, slot],
            kv_send.at[order], kv_recv.at[slot], device(to_plane, copy, to_spot),
        )

    def on_copy(slot, hop):
        return remote(
            got_kv.at[0, slot], got_kv.at[hop, slot], on_send.at[hop - 1, slot],
            on_recv.at[hop - 1, slot], device(plane, lax.rem(copy + hop, copies), spot),
        )

    def back_copy(slot, stage, to_spot):
        return remote(
            out_buf.at[slot], out_ref.at[mine], out_send.at[slot], out_recv.at[mine],
            device(lax.rem(plane + planes - stage, planes), copy, to_spot),
        )

    def back_own():
        return pltpu.make_async_copy(out_buf.at[spot], out_ref.at[mine], out_recv.at[mine])

    def arrive(ref, sem):
        pltpu.make_async_copy(ref, ref, sem).wait()

    barrier = pltpu.get_barrier_semaphore()
    partners = [
        device(lax.rem(plane + stage, planes), copy, lax.rem(spot + step, per_plane))
        for stage in range(planes)
        for step in range(per_plane)
        if stage or step
    ] + [device(plane, lax.rem(copy + hop, copies), spot) for hop in range(1, copies)]
    for partner in partners:
        pl.semaphore_signal(
            barrier, inc=1, device_id=partner, device_id_type=pl.DeviceIdType.MESH
        )
    pltpu.make_async_copy(packed.at[mine, 0], got_q.at[spot], q_recv.at[spot]).start()
    pltpu.make_async_copy(
        packed.at[mine, pl.ds(1, 2)], got_kv.at[0, spot], kv_recv.at[spot]
    ).start()
    peaks[...] = jnp.full_like(peaks, -1e30)
    accums[...] = jnp.zeros_like(accums)
    pl.semaphore_wait(barrier, len(partners))

    def start_stage(make, stage):
        for step in range(per_plane):
            if stage or step:
                make(stage, step).start()

    start_stage(kv_copy, 0)
    start_stage(q_copy, 0)
    for stage in range(1, planes):
        start_stage(q_copy, stage)
    for stage in range(1, planes):
        start_stage(kv_copy, stage)

    def hand_on(stage):
        for i in range(per_plane):
            slot = stage * per_plane + i
            arrive(got_kv.at[0, slot], kv_recv.at[slot])
            for hop in range(1, copies):
                on_copy(slot, hop).start()

    def send_back(stage):
        for i in range(per_plane):
            slot = stage * per_plane + i
            own = jnp.logical_and(stage == 0, spot == i)

            @pl.when(own)
            def _():
                back_own().start()

            @pl.when(jnp.logical_not(own))
            def _():
                back_copy(slot, stage, i).start()

    hand_on(0)

    def step_fn(step, carry):
        stage, turn = step // planes, lax.rem(step, planes)
        last = (stage + 1) // planes
        block = turn + last * (planes - 1 - 2 * turn)

        @pl.when(turn == 0)
        def _():
            for hop in range(1, copies):
                for i in range(per_plane):
                    slot = stage * per_plane + i
                    arrive(got_kv.at[hop, slot], on_recv.at[hop - 1, slot])
            for hop in range(copies):
                for i in range(per_plane):
                    slot = stage * per_plane + i
                    at = (hop * per_plane + i) * width
                    keys[:, at : at + width] = got_kv[hop, slot, 0]
                    wide = jnp.concatenate(
                        [
                            got_kv[hop, slot, 1],
                            jnp.ones((LANES - head, width), jnp.bfloat16),
                        ],
                        axis=0,
                    )
                    values[at : at + width, :] = wide.T

        @pl.when(stage == 0)
        def _():
            for i in range(per_plane):
                slot = block * per_plane + i
                arrive(got_q.at[slot], q_recv.at[slot])

        @pl.when(jnp.logical_and(turn == planes - 1, last == 0))
        def _():
            hand_on(stage + 1)

        @pl.when(jnp.logical_and(turn > 0, last == 1))
        def _():
            send_back(block + 1)

        queries = jnp.concatenate(
            [got_q[block * per_plane + i] for i in range(per_plane)], axis=1
        ).T
        rows = pl.ds(pl.multiple_of(block * stage_rows, stage_rows), stage_rows)
        peak, accum = peaks[rows, :], accums[rows, :]
        for start in range(0, copies * stage_rows, key_step):
            scores = jnp.dot(
                queries, keys[:, start : start + key_step], preferred_element_type=jnp.float32
            )
            peak_new = jnp.maximum(peak, jnp.max(scores, axis=1, keepdims=True))
            terms = jnp.exp2(scores - peak_new).astype(jnp.bfloat16)
            accum = accum * jnp.exp2(peak - peak_new) + jnp.dot(
                terms, values[start : start + key_step, :], preferred_element_type=jnp.float32
            )
            peak = peak_new
        peaks[rows, :] = peak
        accums[rows, :] = accum

        @pl.when(last == 1)
        def _():
            total = accums[rows, :]
            mixed = (total[:, :head] / total[:, head : head + 1]).T.astype(jnp.bfloat16)
            for i in range(per_plane):
                out_buf[block * per_plane + i] = mixed[:, i * width : (i + 1) * width]

        return carry

    lax.fori_loop(0, planes * planes, step_fn, 0)

    for stage in range(planes):
        for step in range(per_plane):
            if stage or step:
                q_copy(stage, step).wait_send()
                kv_copy(stage, step).wait_send()
    send_back(0)
    for slot in range(planes * per_plane):
        for hop in range(1, copies):
            on_copy(slot, hop).wait_send()
    for stage in range(planes):
        for i in range(per_plane):
            slot = stage * per_plane + i
            if stage:
                back_copy(slot, stage, i).wait_send()
            else:

                @pl.when(spot != i)
                def _():
                    back_copy(slot, stage, i).wait_send()

    for slot in range(planes * per_plane):
        arrive(out_ref.at[slot], out_recv.at[slot])


def global_attention(packed, planes, copies, per_plane, key_step):
    heads, _, head, width = packed.shape
    stage_rows = per_plane * width
    rows = planes * stage_rows
    key_step = min(key_step, stage_rows)
    dma = pltpu.SemaphoreType.DMA
    hops = max(1, copies - 1)
    return pl.pallas_call(
        functools.partial(global_kernel, planes, copies, per_plane, key_step),
        in_specs=[pl.BlockSpec(memory_space=pl.ANY)],
        out_specs=pl.BlockSpec(memory_space=pltpu.VMEM),
        out_shape=jax.ShapeDtypeStruct((heads, head, width), jnp.bfloat16),
        scratch_shapes=[
            pltpu.VMEM((heads, head, width), jnp.bfloat16),
            pltpu.VMEM((copies, heads, 2, head, width), jnp.bfloat16),
            pltpu.VMEM((head, copies * stage_rows), jnp.bfloat16),
            pltpu.VMEM((copies * stage_rows, LANES), jnp.bfloat16),
            pltpu.VMEM((rows, 1), jnp.float32),
            pltpu.VMEM((rows, LANES), jnp.float32),
            pltpu.VMEM((heads, head, width), jnp.bfloat16),
            dma((heads,)), dma((heads,)), dma((heads,)), dma((heads,)),
            dma((hops, heads)), dma((hops, heads)), dma((heads,)), dma((heads,)),
        ],
        compiler_params=pltpu.CompilerParams(
            collective_id=0, has_side_effects=True, vmem_limit_bytes=VMEM_BYTES
        ),
        name="global_attention",
    )(packed)


def on_device(tokens, w_qkv_frame, w_out_frame, w_qkv_global, w_out_global):
    view_here, rows_here, model_dim = tokens.shape
    head_size, view_size = lax.axis_size("head"), lax.axis_size("view")
    tokens_here = view_here * rows_here

    shares = head_size // view_here
    cols = model_dim // shares
    share = lax.rem(lax.axis_index("head"), shares)
    sent = jnp.repeat(normalize(tokens), shares, axis=0)
    view_rows = lax.all_to_all(sent, "head", split_axis=0, concat_axis=0, tiled=True)
    view_rows = view_rows.reshape(head_size * rows_here, model_dim)

    def project(which):
        weight = lax.dynamic_slice_in_dim(w_qkv_frame, which * model_dim + share * cols, cols, 1)
        return jnp.dot(view_rows, weight, preferred_element_type=jnp.float32)

    frame_mixed = frame_attention(
        (project(0) * SCORE_SCALE).astype(jnp.bfloat16),
        project(1).astype(jnp.bfloat16),
        project(2).astype(jnp.bfloat16),
    )
    back = lax.all_to_all(
        frame_mixed.reshape(head_size, rows_here, cols), "head", split_axis=0, concat_axis=0, tiled=True
    ).reshape(view_here, shares, rows_here, cols)
    added = jnp.dot(
        jnp.transpose(back, (0, 2, 1, 3)).reshape(tokens_here, model_dim),
        w_out_frame,
        preferred_element_type=jnp.float32,
    )
    after_frame = (tokens.astype(jnp.float32).reshape(tokens_here, model_dim) + added).astype(
        jnp.bfloat16
    )

    heads = model_dim // HEAD
    copies = view_size * head_size // heads
    normed = normalize(after_frame)
    packed = lax.dot_general(
        w_qkv_global, normed, (((0,), (1,)), ((), ())), preferred_element_type=jnp.float32
    ).reshape(3, heads, HEAD, tokens_here)
    scale = jnp.array([SCORE_SCALE, 1.0, 1.0], jnp.float32).reshape(3, 1, 1, 1)
    packed = jnp.transpose((packed * scale).astype(jnp.bfloat16), (1, 0, 2, 3))
    mixed = global_attention(
        packed, view_size // copies, copies, head_size, 1024
    ).reshape(model_dim, tokens_here)
    added = lax.dot_general(
        mixed, w_out_global, (((0,), (0,)), ((), ())), preferred_element_type=jnp.float32
    )
    result = (after_frame.astype(jnp.float32) + added).astype(jnp.bfloat16)
    return result.reshape(view_here, rows_here, model_dim)


def solution(mesh):
    return jax.shard_map(
        on_device,
        mesh=mesh,
        in_specs=(P("view", "head", None), P(), P(), P(), P()),
        out_specs=P("view", "head", None),
        check_vma=False,
    )
```

```python
import functools
import math

import jax
import jax.numpy as jnp
from jax import lax
from jax.experimental import pallas as pl
from jax.experimental.pallas import tpu as pltpu
from jax.sharding import PartitionSpec as P

HEAD = 64
LANES = 128
SCORE_SCALE = HEAD ** (-0.5) * math.log2(math.e)
VMEM_BYTES = 56 * 2**20


def normalize(stream):
    widened = stream.astype(jnp.float32)
    center = jnp.mean(widened, axis=-1, keepdims=True)
    spread = jnp.mean(jnp.square(widened - center), axis=-1, keepdims=True)
    return ((widened - center) * lax.rsqrt(spread + 1e-06)).astype(jnp.bfloat16)


def frame_kernel(
    shares, tokens_ref, weight_ref, back_ref,
    sent, got, weights, packed, out_buf,
    weight_sem, token_send, token_recv, out_send, out_recv,
):
    spots, rows, model_dim = got.shape
    cols = weights.shape[2]
    pairs = cols // LANES
    view, spot = lax.axis_index("view"), lax.axis_index("head")
    share = lax.rem(spot, shares)

    def remote(src, dst, send, recv, to_spot):
        return pltpu.make_async_remote_copy(
            src_ref=src, dst_ref=dst, send_sem=send, recv_sem=recv,
            device_id=(view, to_spot), device_id_type=pl.DeviceIdType.MESH,
        )

    def weight_copy(which):
        at = pl.multiple_of(which * model_dim + share * cols, LANES)
        return pltpu.make_async_copy(
            weight_ref.at[:, pl.ds(at, cols)], weights.at[which], weight_sem.at[which]
        )

    def token_copy(step):
        to_spot = lax.rem(spot + step, spots)
        return remote(
            sent.at[to_spot // shares], got.at[spot], token_send.at[step],
            token_recv.at[spot], to_spot,
        )

    def token_own():
        return pltpu.make_async_copy(sent.at[spot // shares], got.at[spot], token_recv.at[spot])

    def out_copy(pair, step):
        to_spot = lax.rem(spot + step, spots)
        return remote(
            out_buf.at[to_spot, pair], back_ref.at[spot, pair], out_send.at[pair, step],
            out_recv.at[pair, spot], to_spot,
        )

    def out_own(pair):
        return pltpu.make_async_copy(
            out_buf.at[spot, pair], back_ref.at[spot, pair], out_recv.at[pair, spot]
        )

    def arrive(ref, sem):
        pltpu.make_async_copy(ref, ref, sem).wait()

    for which in range(3):
        weight_copy(which).start()
    sent[...] = normalize(tokens_ref[...])
    barrier = pltpu.get_barrier_semaphore()
    for step in range(1, spots):
        pl.semaphore_signal(
            barrier, inc=1, device_id=(view, lax.rem(spot + step, spots)),
            device_id_type=pl.DeviceIdType.MESH,
        )
    pl.semaphore_wait(barrier, spots - 1)
    for step in range(1, spots):
        token_copy(step).start()
    token_own().start()
    for which in range(3):
        weight_copy(which).wait()

    def project(step, carry):
        source = lax.rem(spot + spots - step, spots)
        arrive(got.at[source], token_recv.at[source])
        at = pl.ds(pl.multiple_of(source * rows, rows), rows)
        for which in range(3):
            part = jnp.dot(got[source], weights[which], preferred_element_type=jnp.float32)
            if which == 0:
                part = part * SCORE_SCALE
            packed[which, at, :] = part.astype(jnp.bfloat16)
        return carry

    lax.fori_loop(0, spots, project, 0)

    def send_pair(pair):
        for step in range(1, spots):
            out_copy(pair, step).start()
        out_own(pair).start()

    low = lax.broadcasted_iota(jnp.int32, (spots * rows, LANES), 1) < HEAD
    for pair in range(pairs):
        at = slice(pair * LANES, (pair + 1) * LANES)
        queries, keys, values = packed[0, :, at], packed[1, :, at], packed[2, :, at]
        outs = []
        for mask in (low, jnp.logical_not(low)):
            scores = lax.dot_general(
                queries, jnp.where(mask, keys, 0), (((1,), (1,)), ((), ())),
                preferred_element_type=jnp.float32,
            )
            terms = jnp.exp2(scores - jnp.max(scores, axis=1, keepdims=True))
            outs.append(
                jnp.dot(
                    terms.astype(jnp.bfloat16), jnp.where(mask, values, 1),
                    preferred_element_type=jnp.float32,
                )
            )
        total = jnp.where(low, outs[0][:, LANES - 1 :], outs[1][:, :1])
        mixed = (jnp.where(low, outs[0], outs[1]) / total).astype(jnp.bfloat16)
        for i in range(spots):
            out_buf[i, pair] = mixed[i * rows : (i + 1) * rows]
        if pair:
            send_pair(pair - 1)
    for step in range(1, spots):
        token_copy(step).wait_send()
    send_pair(pairs - 1)
    for pair in range(pairs):
        for step in range(1, spots):
            out_copy(pair, step).wait_send()
        for i in range(spots):
            arrive(back_ref.at[i, pair], out_recv.at[pair, i])


def frame_attention(tokens, weight, spots):
    views, rows, model_dim = tokens.shape
    shares = spots // views
    cols = model_dim // shares
    pairs = cols // LANES
    dma = pltpu.SemaphoreType.DMA
    return pl.pallas_call(
        functools.partial(frame_kernel, shares),
        in_specs=[
            pl.BlockSpec(memory_space=pltpu.VMEM),
            pl.BlockSpec(memory_space=pl.ANY),
        ],
        out_specs=pl.BlockSpec(memory_space=pltpu.VMEM),
        out_shape=jax.ShapeDtypeStruct((spots, pairs, rows, LANES), jnp.bfloat16),
        scratch_shapes=[
            pltpu.VMEM((views, rows, model_dim), jnp.bfloat16),
            pltpu.VMEM((spots, rows, model_dim), jnp.bfloat16),
            pltpu.VMEM((3, model_dim, cols), jnp.bfloat16),
            pltpu.VMEM((3, spots * rows, cols), jnp.bfloat16),
            pltpu.VMEM((spots, pairs, rows, LANES), jnp.bfloat16),
            dma((3,)), dma((spots,)), dma((spots,)),
            dma((pairs, spots)), dma((pairs, spots)),
        ],
        compiler_params=pltpu.CompilerParams(
            collective_id=1, has_side_effects=True, vmem_limit_bytes=VMEM_BYTES
        ),
        name="frame_attention",
    )(tokens, weight)


def project_kernel(
    query_blocks, tokens_ref, back_ref, w_out_ref, w_qkv_ref, after_ref, packed_ref, normed
):
    views, rows, model_dim = tokens_ref.shape
    spots, pairs, _, _ = back_ref.shape
    shares = spots // views

    @pl.when(pl.program_id(0) == 0)
    def _():
        mixed = jnp.concatenate(
            [
                jnp.concatenate(
                    [
                        back_ref[view * shares + share, pair]
                        for share in range(shares)
                        for pair in range(pairs)
                    ],
                    axis=1,
                )
                for view in range(views)
            ],
            axis=0,
        )
        added = jnp.dot(mixed, w_out_ref[...], preferred_element_type=jnp.float32)
        stream = tokens_ref[...].reshape(views * rows, model_dim).astype(jnp.float32)
        after = (stream + added).astype(jnp.bfloat16)
        after_ref[...] = after
        normed[...] = normalize(after)

    part = jnp.dot(normed[...], w_qkv_ref[...], preferred_element_type=jnp.float32)
    part = part * jnp.where(pl.program_id(0) < query_blocks, SCORE_SCALE, 1.0)
    part = part.astype(jnp.bfloat16).T
    for i in range(packed_ref.shape[0]):
        packed_ref[i, 0] = part[i * HEAD : (i + 1) * HEAD]


def project_global(tokens, back, w_out, w_qkv):
    views, rows, model_dim = tokens.shape
    tokens_here = views * rows
    block = 4 * HEAD
    blocks = model_dim // block
    whole = pl.BlockSpec(memory_space=pltpu.VMEM)
    return pl.pallas_call(
        functools.partial(project_kernel, blocks),
        grid=(3 * blocks,),
        in_specs=[whole, whole, whole, pl.BlockSpec((model_dim, block), lambda i: (0, i))],
        out_specs=[
            whole,
            pl.BlockSpec((4, 1, HEAD, tokens_here), lambda i: (i % blocks, i // blocks, 0, 0)),
        ],
        out_shape=[
            jax.ShapeDtypeStruct((tokens_here, model_dim), jnp.bfloat16),
            jax.ShapeDtypeStruct((model_dim // HEAD, 3, HEAD, tokens_here), jnp.bfloat16),
        ],
        scratch_shapes=[pltpu.VMEM((tokens_here, model_dim), jnp.bfloat16)],
        compiler_params=pltpu.CompilerParams(vmem_limit_bytes=VMEM_BYTES),
        name="project_global",
    )(tokens, back, w_out, w_qkv)


def global_kernel(
    planes, copies, per_plane, key_step,
    packed, out_ref,
    got_q, got_kv, keys, values, peaks, accums, out_buf,
    q_send, q_recv, kv_send, kv_recv, on_send, on_recv, out_send, out_recv,
):
    _, _, head, width = packed.shape
    view, spot = lax.axis_index("view"), lax.axis_index("head")
    plane, copy = view // copies, lax.rem(view, copies)
    mine = plane * per_plane + spot
    stage_rows = per_plane * width

    def device(to_plane, to_copy, to_spot):
        return (to_plane * copies + to_copy, to_spot)

    def remote(src, dst, send, recv, target):
        return pltpu.make_async_remote_copy(
            src_ref=src, dst_ref=dst, send_sem=send, recv_sem=recv,
            device_id=target, device_id_type=pl.DeviceIdType.MESH,
        )

    def q_copy(stage, step):
        to_plane, to_spot = lax.rem(plane + stage, planes), lax.rem(spot + step, per_plane)
        slot, order = stage * per_plane + spot, stage * per_plane + step
        return remote(
            packed.at[to_plane * per_plane + to_spot, 0], got_q.at[slot],
            q_send.at[order], q_recv.at[slot], device(to_plane, copy, to_spot),
        )

    def kv_copy(stage, step):
        to_plane, to_spot = lax.rem(plane + stage, planes), lax.rem(spot + step, per_plane)
        slot, order = stage * per_plane + spot, stage * per_plane + step
        return remote(
            packed.at[to_plane * per_plane + to_spot, pl.ds(1, 2)], got_kv.at[0, slot],
            kv_send.at[order], kv_recv.at[slot], device(to_plane, copy, to_spot),
        )

    def on_copy(slot, hop):
        return remote(
            got_kv.at[0, slot], got_kv.at[hop, slot], on_send.at[hop - 1, slot],
            on_recv.at[hop - 1, slot], device(plane, lax.rem(copy + hop, copies), spot),
        )

    def back_copy(slot, stage, to_spot):
        return remote(
            out_buf.at[slot], out_ref.at[mine], out_send.at[slot], out_recv.at[mine],
            device(lax.rem(plane + planes - stage, planes), copy, to_spot),
        )

    def back_own():
        return pltpu.make_async_copy(out_buf.at[spot], out_ref.at[mine], out_recv.at[mine])

    def arrive(ref, sem):
        pltpu.make_async_copy(ref, ref, sem).wait()

    barrier = pltpu.get_barrier_semaphore()
    partners = [
        device(lax.rem(plane + stage, planes), copy, lax.rem(spot + step, per_plane))
        for stage in range(planes)
        for step in range(per_plane)
        if stage or step
    ] + [device(plane, lax.rem(copy + hop, copies), spot) for hop in range(1, copies)]
    for partner in partners:
        pl.semaphore_signal(
            barrier, inc=1, device_id=partner, device_id_type=pl.DeviceIdType.MESH
        )
    pltpu.make_async_copy(packed.at[mine, 0], got_q.at[spot], q_recv.at[spot]).start()
    pltpu.make_async_copy(
        packed.at[mine, pl.ds(1, 2)], got_kv.at[0, spot], kv_recv.at[spot]
    ).start()
    peaks[...] = jnp.full_like(peaks, -1e30)
    accums[...] = jnp.zeros_like(accums)
    pl.semaphore_wait(barrier, len(partners))

    def start_stage(make, stage):
        for step in range(per_plane):
            if stage or step:
                make(stage, step).start()

    start_stage(kv_copy, 0)
    start_stage(q_copy, 0)
    for stage in range(1, planes):
        start_stage(q_copy, stage)
    for stage in range(1, planes):
        start_stage(kv_copy, stage)

    def hand_on(stage):
        for i in range(per_plane):
            slot = stage * per_plane + i
            arrive(got_kv.at[0, slot], kv_recv.at[slot])
            for hop in range(1, copies):
                on_copy(slot, hop).start()

    def send_back(stage):
        for i in range(per_plane):
            slot = stage * per_plane + i
            own = jnp.logical_and(stage == 0, spot == i)

            @pl.when(own)
            def _():
                back_own().start()

            @pl.when(jnp.logical_not(own))
            def _():
                back_copy(slot, stage, i).start()

    hand_on(0)

    def step_fn(step, carry):
        stage, turn = step // planes, lax.rem(step, planes)
        last = (stage + 1) // planes
        block = turn + last * (planes - 1 - 2 * turn)

        @pl.when(turn == 0)
        def _():
            for hop in range(1, copies):
                for i in range(per_plane):
                    slot = stage * per_plane + i
                    arrive(got_kv.at[hop, slot], on_recv.at[hop - 1, slot])
            for hop in range(copies):
                for i in range(per_plane):
                    slot = stage * per_plane + i
                    at = (hop * per_plane + i) * width
                    keys[:, at : at + width] = got_kv[hop, slot, 0]
                    wide = jnp.concatenate(
                        [
                            got_kv[hop, slot, 1],
                            jnp.ones((LANES - head, width), jnp.bfloat16),
                        ],
                        axis=0,
                    )
                    values[at : at + width, :] = wide.T

        @pl.when(stage == 0)
        def _():
            for i in range(per_plane):
                slot = block * per_plane + i
                arrive(got_q.at[slot], q_recv.at[slot])

        @pl.when(jnp.logical_and(turn == planes - 1, last == 0))
        def _():
            hand_on(stage + 1)

        @pl.when(jnp.logical_and(turn > 0, last == 1))
        def _():
            send_back(block + 1)

        queries = jnp.concatenate(
            [got_q[block * per_plane + i] for i in range(per_plane)], axis=1
        ).T
        rows = pl.ds(pl.multiple_of(block * stage_rows, stage_rows), stage_rows)
        peak, accum = peaks[rows, :], accums[rows, :]
        for start in range(0, copies * stage_rows, key_step):
            scores = jnp.dot(
                queries, keys[:, start : start + key_step], preferred_element_type=jnp.float32
            )
            peak_new = jnp.maximum(peak, jnp.max(scores, axis=1, keepdims=True))
            terms = jnp.exp2(scores - peak_new).astype(jnp.bfloat16)
            accum = accum * jnp.exp2(peak - peak_new) + jnp.dot(
                terms, values[start : start + key_step, :], preferred_element_type=jnp.float32
            )
            peak = peak_new
        peaks[rows, :] = peak
        accums[rows, :] = accum

        @pl.when(last == 1)
        def _():
            total = accums[rows, :]
            mixed = (total[:, :head] / total[:, head : head + 1]).T.astype(jnp.bfloat16)
            for i in range(per_plane):
                out_buf[block * per_plane + i] = mixed[:, i * width : (i + 1) * width]

        return carry

    lax.fori_loop(0, planes * planes, step_fn, 0)

    for stage in range(planes):
        for step in range(per_plane):
            if stage or step:
                q_copy(stage, step).wait_send()
                kv_copy(stage, step).wait_send()
    send_back(0)
    for slot in range(planes * per_plane):
        for hop in range(1, copies):
            on_copy(slot, hop).wait_send()
    for stage in range(planes):
        for i in range(per_plane):
            slot = stage * per_plane + i
            if stage:
                back_copy(slot, stage, i).wait_send()
            else:

                @pl.when(spot != i)
                def _():
                    back_copy(slot, stage, i).wait_send()

    for slot in range(planes * per_plane):
        arrive(out_ref.at[slot], out_recv.at[slot])


def global_attention(packed, planes, copies, per_plane, key_step):
    heads, _, head, width = packed.shape
    stage_rows = per_plane * width
    rows = planes * stage_rows
    key_step = min(key_step, stage_rows)
    dma = pltpu.SemaphoreType.DMA
    hops = max(1, copies - 1)
    return pl.pallas_call(
        functools.partial(global_kernel, planes, copies, per_plane, key_step),
        in_specs=[pl.BlockSpec(memory_space=pl.ANY)],
        out_specs=pl.BlockSpec(memory_space=pltpu.VMEM),
        out_shape=jax.ShapeDtypeStruct((heads, head, width), jnp.bfloat16),
        scratch_shapes=[
            pltpu.VMEM((heads, head, width), jnp.bfloat16),
            pltpu.VMEM((copies, heads, 2, head, width), jnp.bfloat16),
            pltpu.VMEM((head, copies * stage_rows), jnp.bfloat16),
            pltpu.VMEM((copies * stage_rows, LANES), jnp.bfloat16),
            pltpu.VMEM((rows, 1), jnp.float32),
            pltpu.VMEM((rows, LANES), jnp.float32),
            pltpu.VMEM((heads, head, width), jnp.bfloat16),
            dma((heads,)), dma((heads,)), dma((heads,)), dma((heads,)),
            dma((hops, heads)), dma((hops, heads)), dma((heads,)), dma((heads,)),
        ],
        compiler_params=pltpu.CompilerParams(
            collective_id=0, has_side_effects=True, vmem_limit_bytes=VMEM_BYTES
        ),
        name="global_attention",
    )(packed)


def on_device(tokens, w_qkv_frame, w_out_frame, w_qkv_global, w_out_global):
    view_here, rows_here, model_dim = tokens.shape
    head_size, view_size = lax.axis_size("head"), lax.axis_size("view")
    tokens_here = view_here * rows_here

    back = frame_attention(tokens, w_qkv_frame, head_size)
    after_frame, packed = project_global(tokens, back, w_out_frame, w_qkv_global)

    copies = view_size * head_size // (model_dim // HEAD)
    mixed = global_attention(
        packed, view_size // copies, copies, head_size, 1024
    ).reshape(model_dim, tokens_here)
    added = lax.dot_general(
        mixed, w_out_global, (((0,), (0,)), ((), ())), preferred_element_type=jnp.float32
    )
    result = (after_frame.astype(jnp.float32) + added).astype(jnp.bfloat16)
    return result.reshape(view_here, rows_here, model_dim)


def solution(mesh):
    return jax.shard_map(
        on_device,
        mesh=mesh,
        in_specs=(P("view", "head", None), P(), P(), P(), P()),
        out_specs=P("view", "head", None),
        check_vma=False,
    )
```

```python
import functools
import math

import jax
import jax.numpy as jnp
from jax import lax
from jax.experimental import pallas as pl
from jax.experimental.pallas import tpu as pltpu
from jax.sharding import PartitionSpec as P

HEAD = 64
LANES = 128
SCORE_SCALE = HEAD ** (-0.5) * math.log2(math.e)
VMEM_BYTES = 56 * 2**20


def normalize(stream):
    widened = stream.astype(jnp.float32)
    center = jnp.mean(widened, axis=-1, keepdims=True)
    spread = jnp.mean(jnp.square(widened - center), axis=-1, keepdims=True)
    return ((widened - center) * lax.rsqrt(spread + 1e-06)).astype(jnp.bfloat16)


def frame_kernel(
    shares, tokens_ref, weight_ref, back_ref,
    sent, got, weights, packed, out_buf,
    weight_sem, token_send, token_recv, out_send, out_recv,
):
    spots, rows, model_dim = got.shape
    cols = weights.shape[2]
    pairs = cols // LANES
    view, spot = lax.axis_index("view"), lax.axis_index("head")
    share = lax.rem(spot, shares)

    def remote(src, dst, send, recv, to_spot):
        return pltpu.make_async_remote_copy(
            src_ref=src, dst_ref=dst, send_sem=send, recv_sem=recv,
            device_id=(view, to_spot), device_id_type=pl.DeviceIdType.MESH,
        )

    def weight_copy(which):
        at = pl.multiple_of(which * model_dim + share * cols, LANES)
        return pltpu.make_async_copy(
            weight_ref.at[:, pl.ds(at, cols)], weights.at[which], weight_sem.at[which]
        )

    def token_copy(step):
        to_spot = lax.rem(spot + step, spots)
        return remote(
            sent.at[to_spot // shares], got.at[spot], token_send.at[step],
            token_recv.at[spot], to_spot,
        )

    def token_own():
        return pltpu.make_async_copy(sent.at[spot // shares], got.at[spot], token_recv.at[spot])

    def out_copy(pair, step):
        to_spot = lax.rem(spot + step, spots)
        return remote(
            out_buf.at[to_spot, pair], back_ref.at[spot, pair], out_send.at[pair, step],
            out_recv.at[pair, spot], to_spot,
        )

    def out_own(pair):
        return pltpu.make_async_copy(
            out_buf.at[spot, pair], back_ref.at[spot, pair], out_recv.at[pair, spot]
        )

    def arrive(ref, sem):
        pltpu.make_async_copy(ref, ref, sem).wait()

    for which in range(3):
        weight_copy(which).start()
    sent[...] = normalize(tokens_ref[...])
    barrier = pltpu.get_barrier_semaphore()
    for step in range(1, spots):
        pl.semaphore_signal(
            barrier, inc=1, device_id=(view, lax.rem(spot + step, spots)),
            device_id_type=pl.DeviceIdType.MESH,
        )
    pl.semaphore_wait(barrier, spots - 1)
    for step in range(1, spots):
        token_copy(step).start()
    token_own().start()
    for which in range(3):
        weight_copy(which).wait()

    def project(step, carry):
        source = lax.rem(spot + spots - step, spots)
        arrive(got.at[source], token_recv.at[source])
        at = pl.ds(pl.multiple_of(source * rows, rows), rows)
        for which in range(3):
            part = jnp.dot(got[source], weights[which], preferred_element_type=jnp.float32)
            if which == 0:
                part = part * SCORE_SCALE
            packed[which, at, :] = part.astype(jnp.bfloat16)
        return carry

    lax.fori_loop(0, spots, project, 0)

    def send_pair(pair):
        for step in range(1, spots):
            out_copy(pair, step).start()
        out_own(pair).start()

    low = lax.broadcasted_iota(jnp.int32, (spots * rows, LANES), 1) < HEAD
    for pair in range(pairs):
        at = slice(pair * LANES, (pair + 1) * LANES)
        queries, keys, values = packed[0, :, at], packed[1, :, at], packed[2, :, at]
        outs = []
        for mask in (low, jnp.logical_not(low)):
            scores = lax.dot_general(
                queries, jnp.where(mask, keys, 0), (((1,), (1,)), ((), ())),
                preferred_element_type=jnp.float32,
            )
            terms = jnp.exp2(scores - jnp.max(scores, axis=1, keepdims=True))
            outs.append(
                jnp.dot(
                    terms.astype(jnp.bfloat16), jnp.where(mask, values, 1),
                    preferred_element_type=jnp.float32,
                )
            )
        total = jnp.where(low, outs[0][:, LANES - 1 :], outs[1][:, :1])
        mixed = (jnp.where(low, outs[0], outs[1]) / total).astype(jnp.bfloat16)
        for i in range(spots):
            out_buf[i, pair] = mixed[i * rows : (i + 1) * rows]
        if pair:
            send_pair(pair - 1)
    for step in range(1, spots):
        token_copy(step).wait_send()
    send_pair(pairs - 1)
    for pair in range(pairs):
        for step in range(1, spots):
            out_copy(pair, step).wait_send()
        for i in range(spots):
            arrive(back_ref.at[i, pair], out_recv.at[pair, i])


def frame_attention(tokens, weight, spots):
    views, rows, model_dim = tokens.shape
    shares = spots // views
    cols = model_dim // shares
    pairs = cols // LANES
    dma = pltpu.SemaphoreType.DMA
    return pl.pallas_call(
        functools.partial(frame_kernel, shares),
        in_specs=[
            pl.BlockSpec(memory_space=pltpu.VMEM),
            pl.BlockSpec(memory_space=pl.ANY),
        ],
        out_specs=pl.BlockSpec(memory_space=pltpu.VMEM),
        out_shape=jax.ShapeDtypeStruct((spots, pairs, rows, LANES), jnp.bfloat16),
        scratch_shapes=[
            pltpu.VMEM((views, rows, model_dim), jnp.bfloat16),
            pltpu.VMEM((spots, rows, model_dim), jnp.bfloat16),
            pltpu.VMEM((3, model_dim, cols), jnp.bfloat16),
            pltpu.VMEM((3, spots * rows, cols), jnp.bfloat16),
            pltpu.VMEM((spots, pairs, rows, LANES), jnp.bfloat16),
            dma((3,)), dma((spots,)), dma((spots,)),
            dma((pairs, spots)), dma((pairs, spots)),
        ],
        compiler_params=pltpu.CompilerParams(
            collective_id=1, has_side_effects=True, vmem_limit_bytes=VMEM_BYTES
        ),
        name="frame_attention",
    )(tokens, weight)


def project_kernel(
    query_blocks, tokens_ref, back_ref, w_out_ref, w_qkv_ref, after_ref, packed_ref, normed
):
    views, rows, model_dim = tokens_ref.shape
    spots, pairs, _, _ = back_ref.shape
    shares = spots // views

    @pl.when(pl.program_id(0) == 0)
    def _():
        mixed = jnp.concatenate(
            [
                jnp.concatenate(
                    [
                        back_ref[view * shares + share, pair]
                        for share in range(shares)
                        for pair in range(pairs)
                    ],
                    axis=1,
                )
                for view in range(views)
            ],
            axis=0,
        )
        added = jnp.dot(mixed, w_out_ref[...], preferred_element_type=jnp.float32)
        stream = tokens_ref[...].reshape(views * rows, model_dim).astype(jnp.float32)
        after = (stream + added).astype(jnp.bfloat16)
        after_ref[...] = after
        normed[...] = normalize(after)

    part = jnp.dot(normed[...], w_qkv_ref[...], preferred_element_type=jnp.float32)
    part = part * jnp.where(pl.program_id(0) < query_blocks, SCORE_SCALE, 1.0)
    part = part.astype(jnp.bfloat16).T
    for i in range(packed_ref.shape[0]):
        packed_ref[i, 0] = part[i * HEAD : (i + 1) * HEAD]


def project_global(tokens, back, w_out, w_qkv):
    views, rows, model_dim = tokens.shape
    tokens_here = views * rows
    block = 4 * HEAD
    blocks = model_dim // block
    whole = pl.BlockSpec(memory_space=pltpu.VMEM)
    return pl.pallas_call(
        functools.partial(project_kernel, blocks),
        grid=(3 * blocks,),
        in_specs=[whole, whole, whole, pl.BlockSpec((model_dim, block), lambda i: (0, i))],
        out_specs=[
            whole,
            pl.BlockSpec((4, 1, HEAD, tokens_here), lambda i: (i % blocks, i // blocks, 0, 0)),
        ],
        out_shape=[
            jax.ShapeDtypeStruct((tokens_here, model_dim), jnp.bfloat16),
            jax.ShapeDtypeStruct((model_dim // HEAD, 3, HEAD, tokens_here), jnp.bfloat16),
        ],
        scratch_shapes=[pltpu.VMEM((tokens_here, model_dim), jnp.bfloat16)],
        compiler_params=pltpu.CompilerParams(vmem_limit_bytes=VMEM_BYTES),
        name="project_global",
    )(tokens, back, w_out, w_qkv)


def global_kernel(
    planes, copies, per_plane, key_step,
    packed, out_ref,
    got_q, got_kv, keys, values, peaks, accums, out_buf,
    q_send, q_recv, kv_send, kv_recv, on_send, on_recv, out_send, out_recv,
):
    _, _, head, width = packed.shape
    view, spot = lax.axis_index("view"), lax.axis_index("head")
    plane, copy = view // copies, lax.rem(view, copies)
    mine = plane * per_plane + spot
    stage_rows = per_plane * width

    def device(to_plane, to_copy, to_spot):
        return (to_plane * copies + to_copy, to_spot)

    def remote(src, dst, send, recv, target):
        return pltpu.make_async_remote_copy(
            src_ref=src, dst_ref=dst, send_sem=send, recv_sem=recv,
            device_id=target, device_id_type=pl.DeviceIdType.MESH,
        )

    def q_copy(stage, step):
        to_plane, to_spot = lax.rem(plane + stage, planes), lax.rem(spot + step, per_plane)
        slot, order = stage * per_plane + spot, stage * per_plane + step
        return remote(
            packed.at[to_plane * per_plane + to_spot, 0], got_q.at[slot],
            q_send.at[order], q_recv.at[slot], device(to_plane, copy, to_spot),
        )

    def kv_copy(stage, step):
        to_plane, to_spot = lax.rem(plane + stage, planes), lax.rem(spot + step, per_plane)
        slot, order = stage * per_plane + spot, stage * per_plane + step
        return remote(
            packed.at[to_plane * per_plane + to_spot, pl.ds(1, 2)], got_kv.at[0, slot],
            kv_send.at[order], kv_recv.at[slot], device(to_plane, copy, to_spot),
        )

    def on_copy(slot, hop):
        return remote(
            got_kv.at[0, slot], got_kv.at[hop, slot], on_send.at[hop - 1, slot],
            on_recv.at[hop - 1, slot], device(plane, lax.rem(copy + hop, copies), spot),
        )

    def back_copy(slot, stage, to_spot):
        return remote(
            out_buf.at[slot], out_ref.at[mine], out_send.at[slot], out_recv.at[mine],
            device(lax.rem(plane + planes - stage, planes), copy, to_spot),
        )

    def back_own():
        return pltpu.make_async_copy(out_buf.at[spot], out_ref.at[mine], out_recv.at[mine])

    def arrive(ref, sem):
        pltpu.make_async_copy(ref, ref, sem).wait()

    barrier = pltpu.get_barrier_semaphore()
    partners = [
        device(lax.rem(plane + stage, planes), copy, lax.rem(spot + step, per_plane))
        for stage in range(planes)
        for step in range(per_plane)
        if stage or step
    ] + [device(plane, lax.rem(copy + hop, copies), spot) for hop in range(1, copies)]
    for partner in partners:
        pl.semaphore_signal(
            barrier, inc=1, device_id=partner, device_id_type=pl.DeviceIdType.MESH
        )
    pltpu.make_async_copy(packed.at[mine, 0], got_q.at[spot], q_recv.at[spot]).start()
    pltpu.make_async_copy(
        packed.at[mine, pl.ds(1, 2)], got_kv.at[0, spot], kv_recv.at[spot]
    ).start()
    peaks[...] = jnp.full_like(peaks, -1e30)
    accums[...] = jnp.zeros_like(accums)
    pl.semaphore_wait(barrier, len(partners))

    def start_stage(make, stage):
        for step in range(per_plane):
            if stage or step:
                make(stage, step).start()

    start_stage(kv_copy, 0)
    start_stage(q_copy, 0)
    for stage in range(1, planes):
        start_stage(q_copy, stage)
    for stage in range(1, planes):
        start_stage(kv_copy, stage)

    def hand_on(stage):
        for i in range(per_plane):
            slot = stage * per_plane + i
            arrive(got_kv.at[0, slot], kv_recv.at[slot])
            for hop in range(1, copies):
                on_copy(slot, hop).start()

    def send_back(stage):
        for i in range(per_plane):
            slot = stage * per_plane + i
            own = jnp.logical_and(stage == 0, spot == i)

            @pl.when(own)
            def _():
                back_own().start()

            @pl.when(jnp.logical_not(own))
            def _():
                back_copy(slot, stage, i).start()

    hand_on(0)

    def step_fn(step, carry):
        stage, turn = step // planes, lax.rem(step, planes)
        last = (stage + 1) // planes
        block = turn + last * (planes - 1 - 2 * turn)

        @pl.when(turn == 0)
        def _():
            for hop in range(1, copies):
                for i in range(per_plane):
                    slot = stage * per_plane + i
                    arrive(got_kv.at[hop, slot], on_recv.at[hop - 1, slot])
            for hop in range(copies):
                for i in range(per_plane):
                    slot = stage * per_plane + i
                    at = (hop * per_plane + i) * width
                    keys[:, at : at + width] = got_kv[hop, slot, 0]
                    wide = jnp.concatenate(
                        [
                            got_kv[hop, slot, 1],
                            jnp.ones((LANES - head, width), jnp.bfloat16),
                        ],
                        axis=0,
                    )
                    values[at : at + width, :] = wide.T

        @pl.when(stage == 0)
        def _():
            for i in range(per_plane):
                slot = block * per_plane + i
                arrive(got_q.at[slot], q_recv.at[slot])

        @pl.when(jnp.logical_and(turn == planes - 1, last == 0))
        def _():
            hand_on(stage + 1)

        @pl.when(jnp.logical_and(turn > 0, last == 1))
        def _():
            send_back(block + 1)

        queries = jnp.concatenate(
            [got_q[block * per_plane + i] for i in range(per_plane)], axis=1
        ).T
        rows = pl.ds(pl.multiple_of(block * stage_rows, stage_rows), stage_rows)
        peak, accum = peaks[rows, :], accums[rows, :]
        for start in range(0, copies * stage_rows, key_step):
            scores = jnp.dot(
                queries, keys[:, start : start + key_step], preferred_element_type=jnp.float32
            )
            peak_new = jnp.maximum(peak, jnp.max(scores, axis=1, keepdims=True))
            terms = jnp.exp2(scores - peak_new).astype(jnp.bfloat16)
            accum = accum * jnp.exp2(peak - peak_new) + jnp.dot(
                terms, values[start : start + key_step, :], preferred_element_type=jnp.float32
            )
            peak = peak_new
        peaks[rows, :] = peak
        accums[rows, :] = accum

        @pl.when(last == 1)
        def _():
            total = accums[rows, :]
            mixed = (total[:, :head] / total[:, head : head + 1]).T.astype(jnp.bfloat16)
            for i in range(per_plane):
                out_buf[block * per_plane + i] = mixed[:, i * width : (i + 1) * width]

        return carry

    lax.fori_loop(0, planes * planes, step_fn, 0)

    for stage in range(planes):
        for step in range(per_plane):
            if stage or step:
                q_copy(stage, step).wait_send()
                kv_copy(stage, step).wait_send()
    send_back(0)
    for slot in range(planes * per_plane):
        for hop in range(1, copies):
            on_copy(slot, hop).wait_send()
    for stage in range(planes):
        for i in range(per_plane):
            slot = stage * per_plane + i
            if stage:
                back_copy(slot, stage, i).wait_send()
            else:

                @pl.when(spot != i)
                def _():
                    back_copy(slot, stage, i).wait_send()

    for slot in range(planes * per_plane):
        arrive(out_ref.at[slot], out_recv.at[slot])


def global_attention(packed, planes, copies, per_plane, key_step):
    heads, _, head, width = packed.shape
    stage_rows = per_plane * width
    rows = planes * stage_rows
    key_step = min(key_step, copies * stage_rows)
    dma = pltpu.SemaphoreType.DMA
    hops = max(1, copies - 1)
    return pl.pallas_call(
        functools.partial(global_kernel, planes, copies, per_plane, key_step),
        in_specs=[pl.BlockSpec(memory_space=pl.ANY)],
        out_specs=pl.BlockSpec(memory_space=pltpu.VMEM),
        out_shape=jax.ShapeDtypeStruct((heads, head, width), jnp.bfloat16),
        scratch_shapes=[
            pltpu.VMEM((heads, head, width), jnp.bfloat16),
            pltpu.VMEM((copies, heads, 2, head, width), jnp.bfloat16),
            pltpu.VMEM((head, copies * stage_rows), jnp.bfloat16),
            pltpu.VMEM((copies * stage_rows, LANES), jnp.bfloat16),
            pltpu.VMEM((rows, 1), jnp.float32),
            pltpu.VMEM((rows, LANES), jnp.float32),
            pltpu.VMEM((heads, head, width), jnp.bfloat16),
            dma((heads,)), dma((heads,)), dma((heads,)), dma((heads,)),
            dma((hops, heads)), dma((hops, heads)), dma((heads,)), dma((heads,)),
        ],
        compiler_params=pltpu.CompilerParams(
            collective_id=0, has_side_effects=True, vmem_limit_bytes=VMEM_BYTES
        ),
        name="global_attention",
    )(packed)


def on_device(tokens, w_qkv_frame, w_out_frame, w_qkv_global, w_out_global):
    view_here, rows_here, model_dim = tokens.shape
    head_size, view_size = lax.axis_size("head"), lax.axis_size("view")
    tokens_here = view_here * rows_here

    back = frame_attention(tokens, w_qkv_frame, head_size)
    after_frame, packed = project_global(tokens, back, w_out_frame, w_qkv_global)

    copies = view_size * head_size // (model_dim // HEAD)
    mixed = global_attention(
        packed, view_size // copies, copies, head_size, 2048
    ).reshape(model_dim, tokens_here)
    added = lax.dot_general(
        mixed, w_out_global, (((0,), (0,)), ((), ())), preferred_element_type=jnp.float32
    )
    result = (after_frame.astype(jnp.float32) + added).astype(jnp.bfloat16)
    return result.reshape(view_here, rows_here, model_dim)


def solution(mesh):
    return jax.shard_map(
        on_device,
        mesh=mesh,
        in_specs=(P("view", "head", None), P(), P(), P(), P()),
        out_specs=P("view", "head", None),
        check_vma=False,
    )
```
